128 devices in a mesh: width: 8 (over y, x_lo), store: 16 (over x_hi, z, core).
Axes of the slice: x: 4 (x_hi: 2, x_lo: 2; x = x_hi * 2 + x_lo), y: 4, z: 4, core: 2. Of those that a mesh axis runs over, the one named last changes fastest.
Arguments:
- activations: bfloat16 [128, 512, 8192], P('store', None, 'width'), may hold values from -6 to 6
- out_grads: bfloat16 [128, 512, 8192], P('store', None, 'width'), may hold values from -6 to 6
- proj_in: bfloat16 [8192, 64], P('width'), may hold values from -0.0625 to 0.0625
- proj_out: bfloat16 [8192, 64], P('width'), may hold values from -0.0625 to 0.0625
- fisher_inv: float32 [4096, 4096], P('store', 'width'), may hold values from -0.09375 to 0.09375
- grad_store: float32 [32768, 4096], P('store', 'width'), may hold values from -6 to 6
Outputs:
- scores: float32 [128, 32768], P('width', 'store')
The draws below stay inside these ranges and needn't reach their ends.
All inputs are finite; a program needn't handle non-finite values.
Results may differ from the reference program's by a relative error of at most 0.0003.
Values sent between devices are 32-bit elements; how exact they have to be, the bound alone decides.
No kernel may reach another device: no remote copies, remote signals or barrier semaphores. Data moves between devices by JAX's collectives and lax.ppermute only.
A program may use at most 128 MiB of HBM per device.

```python
import jax
import jax.numpy as jnp
from jax import lax

D = 8192
RANK = 64
SEQ = 512
COORD = 4096
QUERIES = 128
EXAMPLES = 32768


def block_levels(stream_key, extent, cuts, smallest, largest):
    level, own = 1.0, jax.random.fold_in(stream_key, 6)
    for dim, blocks in cuts:
        steps = jnp.exp(jax.random.uniform(jax.random.fold_in(own, dim), (blocks,), jnp.float32, smallest / len(cuts), largest / len(cuts)))
        level = level * jnp.repeat(steps, extent[dim] // blocks).reshape([-1 if axis == dim else 1 for axis in range(len(extent))])
    return level


def centred(stream_key, extent, scale, limit, shards=(), held_as=jnp.bfloat16):
    loudness = block_levels(stream_key, extent, shards, -0.22, 0.18) if shards else 1.0
    values = jax.random.normal(stream_key, extent, jnp.float32) * scale * loudness
    return jnp.minimum(jnp.maximum(values, -limit), limit).astype(held_as)


def setup_inputs(seed: int = 0) -> dict:
    streams_of = jax.random.split(jax.random.key(seed), 7)
    activations = centred(streams_of[0], (QUERIES, SEQ, D), 1.0, 6.0, ((0, 16), (2, 8)))
    out_grads = centred(streams_of[1], (QUERIES, SEQ, D), 1.0, 6.0, ((0, 16), (2, 8)))
    proj_in = centred(streams_of[2], (D, RANK), D ** -0.5, 0.0625, ((0, 8),))
    proj_out = centred(streams_of[3], (D, RANK), D ** -0.5, 0.0625, ((0, 8),))
    fisher_inv = centred(streams_of[4], (COORD, COORD), COORD ** -0.5, 0.09375, ((0, 16), (1, 8)), jnp.float32)
    grad_store = centred(streams_of[5], (EXAMPLES, COORD), 1.0, 6.0, ((0, 16), (1, 8)), jnp.float32)
    return dict(activations=activations, out_grads=out_grads, proj_in=proj_in, proj_out=proj_out, fisher_inv=fisher_inv, grad_store=grad_store)


def reference(activations, out_grads, proj_in, proj_out, fisher_inv, grad_store):
    queries = activations.shape[0]
    act_proj = jnp.dot(activations.reshape(-1, D), proj_in, preferred_element_type=jnp.float32).reshape(queries, SEQ, RANK)
    grad_proj = jnp.dot(out_grads.reshape(-1, D), proj_out, preferred_element_type=jnp.float32).reshape(queries, SEQ, RANK)
    gradient = jnp.einsum("qti,qtj->qij", grad_proj, act_proj, precision=lax.Precision.HIGHEST) / SEQ
    gradient = gradient.reshape(queries, COORD)
    precond = jnp.dot(gradient, fisher_inv, precision=lax.Precision.HIGHEST)
    return jnp.dot(precond, grad_store.T, precision=lax.Precision.HIGHEST)
```

```python
import jax
import jax.numpy as jnp
from jax import lax
from jax.experimental import pallas as pl
from jax.experimental.pallas import tpu as pltpu
from jax.sharding import PartitionSpec as P

RANK = 64
SEQ = 512
COORD = 4096
WIDTH = 8
STORE = 16


NT = (((1,), (1,)), ((), ()))
NN = (((1,), (0,)), ((), ()))


def split(x):
    high = x.astype(jnp.bfloat16)
    low = (x - high.astype(jnp.float32)).astype(jnp.bfloat16)
    return high, low


def dot(a, b, dims):
    return lax.dot_general(a, b, dims, preferred_element_type=jnp.float32)


def dot3(a, b, dims):
    a_high, a_low = split(a)
    b_high, b_low = split(b)
    return dot(a_high, b_high, dims) + (dot(a_high, b_low, dims) + dot(a_low, b_high, dims))


def project_kernel(query_ref, act_ref, grad_ref, in_ref, out_ref, result_ref):
    result_ref[:RANK, :] = dot(out_ref[...], grad_ref[0], NT)
    result_ref[RANK:, :] = dot(in_ref[...], act_ref[0], NT)


def project(query, activations, out_grads, proj_in_t, proj_out_t):
    depth = activations.shape[2]
    block = 256
    tokens = pl.BlockSpec((1, block, depth), lambda t, query: (query[0], t, 0))
    weights = pl.BlockSpec((RANK, depth), lambda t, query: (0, 0))
    return pl.pallas_call(
        project_kernel,
        out_shape=jax.ShapeDtypeStruct((2 * RANK, SEQ), jnp.float32),
        grid_spec=pltpu.PrefetchScalarGridSpec(
            num_scalar_prefetch=1,
            grid=(SEQ // block,),
            in_specs=[tokens, tokens, weights, weights],
            out_specs=pl.BlockSpec((2 * RANK, block), lambda t, query: (0, t)),
        ),
        cost_estimate=pl.CostEstimate(
            flops=4 * SEQ * depth * RANK, bytes_accessed=4 * SEQ * depth, transcendentals=0
        ),
        name="project",
    )(query, activations, out_grads, proj_in_t, proj_out_t)


def gradient_kernel(*refs):
    *parts, result_ref, held = refs
    total = parts[0][...]
    for part in parts[1:]:
        total = total + part[...]
    held[...] = dot3(total[:RANK], total[RANK:], NT) * (1.0 / SEQ)
    pairs = jnp.concatenate(
        [held[pl.ds(0, RANK // 2, stride=2), :], held[pl.ds(1, RANK // 2, stride=2), :]], axis=1
    )
    rows = jnp.broadcast_to(pairs.reshape(STORE, 1, 2, 128), (STORE, WIDTH, 2, 128))
    result_ref[...] = rows.reshape(STORE * WIDTH, 2, 128)


def gradient(parts):
    return pl.pallas_call(
        gradient_kernel,
        out_shape=jax.ShapeDtypeStruct((STORE * WIDTH, 2, 128), jnp.float32),
        scratch_shapes=[pltpu.VMEM((RANK, RANK), jnp.float32)],
        name="gradient",
    )(*parts)


def partial_kernel(rows_ref, fisher_ref, result_ref):
    total = dot3(rows_ref[:, 0, :], fisher_ref[:128, :], NN)
    total = total + dot3(rows_ref[:, 1, :], fisher_ref[128:, :], NN)
    result_ref[...] = total.reshape(result_ref.shape)


def partial_precond(rows, fisher):
    columns = fisher.shape[1]
    return pl.pallas_call(
        partial_kernel,
        out_shape=jax.ShapeDtypeStruct((STORE, WIDTH, columns), jnp.float32),
        name="partial_precond",
    )(rows, fisher)


def total_kernel(parts_ref, result_ref):
    total = jnp.sum(parts_ref[...], axis=0, keepdims=True)
    result_ref[...] = jnp.broadcast_to(total, result_ref.shape)


def total_precond(parts):
    return pl.pallas_call(
        total_kernel, out_shape=jax.ShapeDtypeStruct(parts.shape, jnp.float32), name="total_precond"
    )(parts)


def split_kernel(x_ref, high_ref, low_ref):
    high_ref[...], low_ref[...] = split(x_ref[...])


def split_store(store):
    rows, columns = store.shape
    block = pl.BlockSpec((rows // 4, columns), lambda i: (i, 0))
    halves = jax.ShapeDtypeStruct(store.shape, jnp.bfloat16)
    return pl.pallas_call(
        split_kernel,
        out_shape=(halves, halves),
        grid=(4,),
        in_specs=[block],
        out_specs=(block, block),
        name="split_store",
    )(store)


def score_kernel(me_ref, precond_ref, high_ref, low_ref, *refs):
    *result_refs, p_high, p_low = refs
    rows = 16
    columns = precond_ref.shape[2]
    for k in range(WIDTH):
        owner = me_ref[0] ^ k
        block = precond_ref[pl.ds(2 * owner, 2)].reshape(rows, columns)
        p_high[k * rows : (k + 1) * rows, :], p_low[k * rows : (k + 1) * rows, :] = split(block)
    a_high, a_low = p_high[...], p_low[...]
    width = 512
    for n in range(high_ref.shape[0] // width):
        span = slice(n * width, (n + 1) * width)
        b_high, b_low = high_ref[span, :], low_ref[span, :]
        total = dot(a_high, b_high, NT) + (dot(a_high, b_low, NT) + dot(a_low, b_high, NT))
        for k in range(WIDTH):
            result_refs[k][:, span] = total[k * rows : (k + 1) * rows, :]


def scores(me, precond, high, low):
    examples, columns = high.shape
    block = jax.ShapeDtypeStruct((16, examples), jnp.float32)
    vmem = pl.BlockSpec(memory_space=pltpu.VMEM)
    return pl.pallas_call(
        score_kernel,
        out_shape=(block,) * WIDTH,
        in_specs=[pl.BlockSpec(memory_space=pltpu.SMEM), vmem, vmem, vmem],
        out_specs=(vmem,) * WIDTH,
        scratch_shapes=[pltpu.VMEM((128, columns), jnp.bfloat16)] * 2,
        name="scores",
    )(me, precond, high, low)


def exchange(x, k):
    return lax.ppermute(x, "width", [(i, i ^ k) for i in range(WIDTH)])


ORDER = (5, 3, 7, 1, 4, 6, 2)


def body(activations, out_grads, proj_in, proj_out, fisher_inv, grad_store):
    me = lax.axis_index("width")
    proj_in_t, proj_out_t = proj_in.T, proj_out.T
    received = []
    for k in ORDER:
        part = project((me ^ k)[None], activations, out_grads, proj_in_t, proj_out_t)
        received.append(exchange(part, k))
    own = project(me[None], activations, out_grads, proj_in_t, proj_out_t)
    high, low = split_store(grad_store)
    outgoing = gradient([own] + received)
    rows = lax.all_to_all(outgoing, ("store", "width"), 0, 0)
    parts = lax.all_to_all(partial_precond(rows, fisher_inv), "store", 0, 0)
    precond = lax.all_to_all(total_precond(parts), "store", 0, 0)
    blocks = scores(me[None], precond, high, low)
    total = blocks[0]
    for block in [exchange(blocks[k], k) for k in ORDER]:
        total = total + block
    return total


def solution(mesh):
    placed = (
        P("store", None, "width"),
        P("store", None, "width"),
        P("width", None),
        P("width", None),
        P("store", "width"),
        P("store", "width"),
    )
    return jax.shard_map(
        body, mesh=mesh, in_specs=placed, out_specs=P("width", "store"), check_vma=False
    )
```

```python
import functools

import jax
import jax.numpy as jnp
from jax import lax
from jax.experimental import pallas as pl
from jax.experimental.pallas import tpu as pltpu
from jax.sharding import PartitionSpec as P

RANK = 64
SEQ = 512
WIDTH = 8
STORE = 16
NEAR = 8
MIB = 1024 * 1024


NT = (((1,), (1,)), ((), ()))
NN = (((1,), (0,)), ((), ()))


def split(x):
    high = x.astype(jnp.bfloat16)
    low = (x - high.astype(jnp.float32)).astype(jnp.bfloat16)
    return high, low


def dot(a, b, dims):
    return lax.dot_general(a, b, dims, preferred_element_type=jnp.float32)


def dot3(a, b, dims):
    a_high, a_low = split(a)
    b_high, b_low = split(b)
    return dot(a_high, b_high, dims) + (dot(a_high, b_low, dims) + dot(a_low, b_high, dims))


def limit(mib):
    return pltpu.CompilerParams(vmem_limit_bytes=mib * MIB)


def hbm(x):
    return pltpu.with_memory_space_constraint(x, pltpu.HBM)


VMEM = pl.BlockSpec(memory_space=pltpu.VMEM)
SMEM = pl.BlockSpec(memory_space=pltpu.SMEM)
HBM = pl.BlockSpec(memory_space=pltpu.HBM)


def project_first_kernel(k, place_ref, act_ref, grad_ref, in_ref, out_ref, *refs):
    result_ref, tokens, weights, token_sem, weight_sem = refs
    weight_copies = [
        pltpu.make_async_copy(source, weights.at[side], weight_sem.at[side])
        for side, source in enumerate((out_ref, in_ref))
    ]
    copies = [
        pltpu.make_async_copy(source.at[place_ref[0] ^ k], tokens.at[side], token_sem.at[side])
        for side, source in enumerate((grad_ref, act_ref))
    ]
    for copy in weight_copies + copies:
        copy.start()
    for side in range(2):
        weight_copies[side].wait()
        copies[side].wait()
        result_ref[side * RANK : (side + 1) * RANK, :] = dot(weights[side], tokens[side], NT)


def project_first(k, place, activations, out_grads, proj_in_t, proj_out_t):
    depth = activations.shape[2]
    return pl.pallas_call(
        functools.partial(project_first_kernel, k),
        out_shape=jax.ShapeDtypeStruct((2 * RANK, SEQ), jnp.float32),
        in_specs=[SMEM, HBM, HBM, HBM, HBM],
        out_specs=VMEM,
        scratch_shapes=[
            pltpu.VMEM((2, SEQ, depth), jnp.bfloat16),
            pltpu.VMEM((2, RANK, depth), jnp.bfloat16),
            pltpu.SemaphoreType.DMA((2,)),
            pltpu.SemaphoreType.DMA((2,)),
        ],
        compiler_params=limit(6),
        cost_estimate=project_cost(1, depth),
        name="project_first",
    )(place, hbm(activations), hbm(out_grads), hbm(proj_in_t), hbm(proj_out_t))


def project_cost(count, depth):
    return pl.CostEstimate(
        flops=4 * count * SEQ * depth * RANK,
        bytes_accessed=4 * count * SEQ * depth,
        transcendentals=0,
    )


def project_kernel(group, place_ref, act_ref, grad_ref, in_ref, out_ref, *result_refs):
    for k, result_ref in zip(group, result_refs, strict=True):
        query = place_ref[0] ^ k
        result_ref[:RANK, :] = dot(out_ref[...], grad_ref[query], NT)
        result_ref[RANK:, :] = dot(in_ref[...], act_ref[query], NT)


def project(group, place, activations, out_grads, proj_in_t, proj_out_t):
    count = len(group)
    part = jax.ShapeDtypeStruct((2 * RANK, SEQ), jnp.float32)
    return pl.pallas_call(
        functools.partial(project_kernel, group),
        out_shape=(part,) * count,
        in_specs=[SMEM, VMEM, VMEM, VMEM, VMEM],
        out_specs=(VMEM,) * count,
        compiler_params=limit(20),
        cost_estimate=project_cost(count, activations.shape[2]),
        name="project",
    )(place, activations, out_grads, proj_in_t, proj_out_t)


def gradient_kernel(place_ref, *refs):
    *parts, result_ref, held = refs
    total = parts[0][...]
    for part in parts[1:]:
        total = total + part[...]
    held[...] = dot3(total[:RANK], total[RANK:], NT) * (1.0 / SEQ)
    half = RANK // 2
    pairs = jnp.concatenate(
        [held[pl.ds(0, half, stride=2), :], held[pl.ds(1, half, stride=2), :]], axis=1
    )
    row = lax.broadcasted_iota(jnp.int32, pairs.shape, 0)
    for bit in (1, 2, 4):
        far = 2 * bit
        swapped = jnp.where(
            (row & far) == 0, pltpu.roll(pairs, half - far, 0), pltpu.roll(pairs, far, 0)
        )
        pairs = jnp.where((place_ref[1] & bit) != 0, swapped, pairs)
    for side in range(2):
        block = pairs[side * 16 : (side + 1) * 16, :]
        for i in range(WIDTH):
            result_ref[side * WIDTH + i] = block


def gradient(place, parts):
    return pl.pallas_call(
        gradient_kernel,
        out_shape=jax.ShapeDtypeStruct((2 * WIDTH, 16, 128), jnp.float32),
        in_specs=[SMEM] + [VMEM] * len(parts),
        out_specs=VMEM,
        scratch_shapes=[pltpu.VMEM((RANK, RANK), jnp.float32)],
        compiler_params=limit(4),
        name="gradient",
    )(place, *parts)


def partial_kernel(rows_ref, *refs):
    *fisher_refs, result_ref = refs
    high, low = split(rows_ref[...])
    total = None
    for i, fisher_ref in enumerate(fisher_refs):
        f_high, f_low = split(fisher_ref[...])
        for side in range(2):
            rows = 2 * i + side
            span = slice(side * 128, (side + 1) * 128)
            a_high, a_low = high[:, rows, :], low[:, rows, :]
            term = dot(a_high, f_high[span], NN) + (
                dot(a_high, f_low[span], NN) + dot(a_low, f_high[span], NN)
            )
            total = term if total is None else total + term
    for i in range(STORE):
        result_ref[i] = total


def partial_precond(rows, fisher):
    columns = fisher[0].shape[1]
    return pl.pallas_call(
        partial_kernel,
        out_shape=jax.ShapeDtypeStruct((STORE, 2 * WIDTH, columns), jnp.float32),
        in_specs=[VMEM] * (1 + len(fisher)),
        out_specs=VMEM,
        compiler_params=limit(10),
        name="partial_precond",
    )(rows, *fisher)


def score_kernel(place_ref, halves_ref, store_ref, *refs):
    *result_refs, p_high, p_low = refs
    rows = 8
    for k in range(WIDTH):
        owner = place_ref[0] ^ k
        offset = pl.ds(pl.multiple_of((owner >> 2) * rows, rows), rows)
        for core in range(2):
            near = ((2 * owner) & (NEAR - 1)) + core
            block = halves_ref[near, offset, :] + halves_ref[NEAR + near, offset, :]
            span = slice((2 * k + core) * rows, (2 * k + core + 1) * rows)
            p_high[span, :] = block.astype(jnp.bfloat16).astype(jnp.float32)
            p_low[span, :] = block - p_high[span, :]
    a_high = p_high[...].astype(jnp.bfloat16)
    a_low = p_low[...].astype(jnp.bfloat16)
    width = 512
    for n in range(store_ref.shape[0] // width):
        span = slice(n * width, (n + 1) * width)
        b_high, b_low = split(store_ref[span, :])
        total = dot(a_high, b_high, NT) + (dot(a_high, b_low, NT) + dot(a_low, b_high, NT))
        for k in range(WIDTH):
            result_refs[k][:, span] = total[16 * k : 16 * (k + 1), :]


def scores(place, halves, store):
    examples, columns = store.shape
    block = jax.ShapeDtypeStruct((16, examples), jnp.float32)
    return pl.pallas_call(
        score_kernel,
        out_shape=(block,) * WIDTH,
        in_specs=[SMEM, VMEM, VMEM],
        out_specs=(VMEM,) * WIDTH,
        scratch_shapes=[pltpu.VMEM((128, columns), jnp.float32)] * 2,
        compiler_params=limit(12),
        name="scores",
    )(place, halves, store)


def exchange(x, axis, k, size):
    return lax.ppermute(x, axis, [(i, i ^ k) for i in range(size)])


ORDER = (5, 3, 7, 1, 4, 6, 2)
GROUPS = (((5,), 4), ((3,), 2), ((7, 1), 6), ((4, 6), 0), ((2,), 0), ((0,), 0))


def body(activations, out_grads, proj_in, proj_out, fisher_inv, grad_store):
    place = jnp.stack([lax.axis_index("width"), lax.axis_index("store") & (NEAR - 1)])
    proj_in_t, proj_out_t = proj_in.T, proj_out.T
    weights = (activations, out_grads, proj_in_t, proj_out_t)
    parts, fisher = {}, {0: fisher_inv}
    for n, (group, far) in enumerate(GROUPS):
        if n:
            projected = project(group, place, *weights)
        else:
            projected = (project_first(group[0], place, *weights),)
        for k, part in zip(group, projected, strict=True):
            parts[k] = exchange(part, "width", k, WIDTH) if k else part
        if far:
            fisher[far] = exchange(fisher_inv, "store", far, STORE)
    last, *blocks = lax.optimization_barrier((parts[0], *(fisher[k] for k in (0, 2, 4, 6))))
    for k, block in zip((0, 2, 4, 6), blocks, strict=True):
        fisher[k + 1] = exchange(block, "store", 1, STORE)
    outgoing = gradient(place, [parts[k] for k in range(WIDTH)])
    groups = [
        [(side * NEAR + i) * WIDTH + w for side in range(2) for w in range(WIDTH)]
        for i in range(NEAR)
    ]
    rows = lax.all_to_all(outgoing, ("store", "width"), 0, 0, axis_index_groups=groups)
    halves = partial_precond(rows, [fisher[i] for i in range(NEAR)])
    halves = lax.all_to_all(halves, "store", 0, 0)
    blocks = scores(place, halves, grad_store)
    total = blocks[0]
    for block in [exchange(blocks[k], "width", k, WIDTH) for k in ORDER]:
        total = total + block
    return total


def solution(mesh):
    placed = (
        P("store", None, "width"),
        P("store", None, "width"),
        P("width", None),
        P("width", None),
        P("store", "width"),
        P("store", "width"),
    )
    return jax.shard_map(
        body, mesh=mesh, in_specs=placed, out_specs=P("width", "store"), check_vma=False
    )
```

```python
import functools

import jax
import jax.numpy as jnp
from jax import lax
from jax.experimental import pallas as pl
from jax.experimental.pallas import tpu as pltpu
from jax.sharding import PartitionSpec as P

RANK = 64
SEQ = 512
WIDTH = 8
STORE = 16
NEAR = 8
MIB = 1024 * 1024


NT = (((1,), (1,)), ((), ()))
NN = (((1,), (0,)), ((), ()))


def split(x):
    high = x.astype(jnp.bfloat16)
    low = (x - high.astype(jnp.float32)).astype(jnp.bfloat16)
    return high, low


def dot(a, b, dims):
    return lax.dot_general(a, b, dims, preferred_element_type=jnp.float32)


def dot3(a, b, dims):
    a_high, a_low = split(a)
    b_high, b_low = split(b)
    return dot(a_high, b_high, dims) + (dot(a_high, b_low, dims) + dot(a_low, b_high, dims))


def limit(mib):
    return pltpu.CompilerParams(vmem_limit_bytes=mib * MIB)


def hbm(x):
    return pltpu.with_memory_space_constraint(x, pltpu.HBM)


VMEM = pl.BlockSpec(memory_space=pltpu.VMEM)
SMEM = pl.BlockSpec(memory_space=pltpu.SMEM)
HBM = pl.BlockSpec(memory_space=pltpu.HBM)


def project_first_kernel(k, place_ref, act_ref, grad_ref, in_ref, out_ref, *refs):
    result_ref, tokens, weights, token_sem, weight_sem = refs
    weight_copies = [
        pltpu.make_async_copy(source, weights.at[side], weight_sem.at[side])
        for side, source in enumerate((out_ref, in_ref))
    ]
    copies = [
        pltpu.make_async_copy(source.at[place_ref[0] ^ k], tokens.at[side], token_sem.at[side])
        for side, source in enumerate((grad_ref, act_ref))
    ]
    for copy in weight_copies + copies:
        copy.start()
    for side in range(2):
        weight_copies[side].wait()
        copies[side].wait()
        result_ref[side * RANK : (side + 1) * RANK, :] = dot(weights[side], tokens[side], NT)


def project_first(k, place, activations, out_grads, proj_in_t, proj_out_t):
    depth = activations.shape[2]
    return pl.pallas_call(
        functools.partial(project_first_kernel, k),
        out_shape=jax.ShapeDtypeStruct((2 * RANK, SEQ), jnp.float32),
        in_specs=[SMEM, HBM, HBM, HBM, HBM],
        out_specs=VMEM,
        scratch_shapes=[
            pltpu.VMEM((2, SEQ, depth), jnp.bfloat16),
            pltpu.VMEM((2, RANK, depth), jnp.bfloat16),
            pltpu.SemaphoreType.DMA((2,)),
            pltpu.SemaphoreType.DMA((2,)),
        ],
        compiler_params=limit(6),
        cost_estimate=project_cost(1, depth),
        name="project_first",
    )(place, hbm(activations), hbm(out_grads), hbm(proj_in_t), hbm(proj_out_t))


def project_cost(count, depth):
    return pl.CostEstimate(
        flops=4 * count * SEQ * depth * RANK,
        bytes_accessed=4 * count * SEQ * depth,
        transcendentals=0,
    )


def project_kernel(group, place_ref, act_ref, grad_ref, in_ref, out_ref, *result_refs):
    for k, result_ref in zip(group, result_refs, strict=True):
        query = place_ref[0] ^ k
        result_ref[:RANK, :] = dot(out_ref[...], grad_ref[query], NT)
        result_ref[RANK:, :] = dot(in_ref[...], act_ref[query], NT)


def project(group, place, activations, out_grads, proj_in_t, proj_out_t):
    count = len(group)
    part = jax.ShapeDtypeStruct((2 * RANK, SEQ), jnp.float32)
    return pl.pallas_call(
        functools.partial(project_kernel, group),
        out_shape=(part,) * count,
        in_specs=[SMEM, VMEM, VMEM, VMEM, VMEM],
        out_specs=(VMEM,) * count,
        compiler_params=limit(20),
        cost_estimate=project_cost(count, activations.shape[2]),
        name="project",
    )(place, activations, out_grads, proj_in_t, proj_out_t)


def gradient_kernel(place_ref, *refs):
    *parts, result_ref, held = refs
    total = parts[0][...]
    for part in parts[1:]:
        total = total + part[...]
    held[...] = dot3(total[:RANK], total[RANK:], NT) * (1.0 / SEQ)
    half = RANK // 2
    pairs = jnp.concatenate(
        [held[pl.ds(0, half, stride=2), :], held[pl.ds(1, half, stride=2), :]], axis=1
    )
    row = lax.broadcasted_iota(jnp.int32, pairs.shape, 0)
    for bit in (1, 2, 4):
        far = 2 * bit
        swapped = jnp.where(
            (row & far) == 0, pltpu.roll(pairs, half - far, 0), pltpu.roll(pairs, far, 0)
        )
        pairs = jnp.where((place_ref[1] & bit) != 0, swapped, pairs)
    for side in range(2):
        block = pairs[side * 16 : (side + 1) * 16, :]
        for i in range(WIDTH):
            result_ref[side * WIDTH + i] = block


def gradient(place, parts):
    return pl.pallas_call(
        gradient_kernel,
        out_shape=jax.ShapeDtypeStruct((2 * WIDTH, 16, 128), jnp.float32),
        in_specs=[SMEM] + [VMEM] * len(parts),
        out_specs=VMEM,
        scratch_shapes=[pltpu.VMEM((RANK, RANK), jnp.float32)],
        compiler_params=limit(4),
        name="gradient",
    )(place, *parts)


def partial_kernel(rows_ref, *refs):
    *fisher_refs, result_ref = refs
    total = None
    for i, fisher_ref in enumerate(fisher_refs):
        rows = jnp.concatenate([rows_ref[:, 2 * i, :], rows_ref[:, 2 * i + 1, :]], axis=1)
        high, low = split(rows)
        f_high, f_low = split(fisher_ref[...])
        half = rows.shape[0]
        wide = dot(jnp.concatenate([high, low], axis=0), f_high, NN)
        term = wide[:half] + (wide[half:] + dot(high, f_low, NN))
        total = term if total is None else total + term
    for i in range(STORE // 2):
        result_ref[i] = total


def partial_precond(rows, fisher):
    columns = fisher[0].shape[1]
    return pl.pallas_call(
        partial_kernel,
        out_shape=jax.ShapeDtypeStruct((STORE // 2, 2 * WIDTH, columns), jnp.float32),
        in_specs=[VMEM] * (1 + len(fisher)),
        out_specs=VMEM,
        compiler_params=limit(10),
        name="partial_precond",
    )(rows, *fisher)


def split_kernel(store_ref, high_ref, low_ref):
    high_ref[...], low_ref[...] = split(store_ref[...])


def split_store(store):
    half = jax.ShapeDtypeStruct(store.shape, jnp.bfloat16)
    return pl.pallas_call(
        split_kernel,
        out_shape=(half, half),
        in_specs=[VMEM],
        out_specs=(VMEM, VMEM),
        compiler_params=limit(12),
        name="split_store",
    )(store)


def score_kernel(place_ref, own_ref, other_ref, high_ref, low_ref, *refs):
    *result_refs, parts = refs
    rows = 8
    half = 2 * WIDTH * rows
    for k in range(WIDTH):
        owner = place_ref[0] ^ k
        z = owner & 3
        offset = pl.ds(pl.multiple_of((owner >> 2) * rows, rows), rows)
        for swap, halves_ref in enumerate((own_ref, other_ref)):
            core = (place_ref[1] & 1) ^ swap
            block = halves_ref[z, offset, :] + halves_ref[4 + z, offset, :]
            start = pl.multiple_of((2 * k + core) * rows, rows)
            high = block.astype(jnp.bfloat16).astype(jnp.float32)
            parts[pl.ds(start, rows), :] = high
            parts[pl.ds(start + half, rows), :] = block - high
    both = parts[...].astype(jnp.bfloat16)
    width = 512
    for n in range(high_ref.shape[0] // width):
        span = slice(n * width, (n + 1) * width)
        wide = dot(both, high_ref[span, :], NT)
        total = wide[:half] + (wide[half:] + dot(both[:half], low_ref[span, :], NT))
        for k in range(WIDTH):
            result_refs[k][:, span] = total[16 * k : 16 * (k + 1), :]


def scores(place, own, other, high, low):
    examples, columns = high.shape
    block = jax.ShapeDtypeStruct((16, examples), jnp.float32)
    return pl.pallas_call(
        score_kernel,
        out_shape=(block,) * WIDTH,
        in_specs=[SMEM, VMEM, VMEM, VMEM, VMEM],
        out_specs=(VMEM,) * WIDTH,
        scratch_shapes=[pltpu.VMEM((256, columns), jnp.float32)],
        compiler_params=limit(12),
        name="scores",
    )(place, own, other, high, low)


def exchange(x, axis, k, size):
    return lax.ppermute(x, axis, [(i, i ^ k) for i in range(size)])


ORDER = (5, 4, 3, 7, 6, 2, 1)
GROUPS = (((5,), (4, 2)), ((4,), (6,)), ((3, 7), ()), ((6, 2), ()), ((1,), ()), ((0,), ()))


def body(activations, out_grads, proj_in, proj_out, fisher_inv, grad_store):
    place = jnp.stack([lax.axis_index("width"), lax.axis_index("store") & (NEAR - 1)])
    proj_in_t, proj_out_t = proj_in.T, proj_out.T
    weights = (activations, out_grads, proj_in_t, proj_out_t)
    parts, fisher = {}, {0: fisher_inv}
    for n, (group, around) in enumerate(GROUPS):
        if n:
            projected = project(group, place, *weights)
        else:
            projected = (project_first(group[0], place, *weights),)
        for k, part in zip(group, projected, strict=True):
            parts[k] = exchange(part, "width", k, WIDTH) if k else part
        for far in around:
            fisher[far] = exchange(fisher_inv, "store", far, STORE)
    last, *blocks = lax.optimization_barrier((parts[0], *(fisher[k] for k in (0, 2, 4, 6))))
    for k, block in zip((0, 2, 4, 6), blocks, strict=True):
        fisher[k + 1] = exchange(block, "store", 1, STORE)
    store, _ = lax.optimization_barrier((grad_store, parts[0]))
    high, low = split_store(store)
    outgoing = gradient(place, [parts[k] for k in range(WIDTH)])
    groups = [
        [(side * NEAR + i) * WIDTH + w for side in range(2) for w in range(WIDTH)]
        for i in range(NEAR)
    ]
    rows = lax.all_to_all(outgoing, ("store", "width"), 0, 0, axis_index_groups=groups)
    halves = partial_precond(rows, [fisher[i] for i in range(NEAR)])
    cores = [list(range(core, STORE, 2)) for core in range(2)]
    halves = lax.all_to_all(halves, "store", 0, 0, axis_index_groups=cores)
    blocks = scores(place, halves, exchange(halves, "store", 1, STORE), high, low)
    total = blocks[0]
    for block in [exchange(blocks[k], "width", k, WIDTH) for k in ORDER]:
        total = total + block
    return total


def solution(mesh):
    placed = (
        P("store", None, "width"),
        P("store", None, "width"),
        P("width", None),
        P("width", None),
        P("store", "width"),
        P("store", "width"),
    )
    return jax.shard_map(
        body, mesh=mesh, in_specs=placed, out_specs=P("width", "store"), check_vma=False
    )
```

```python
import functools

import jax
import jax.numpy as jnp
from jax import lax
from jax.experimental import pallas as pl
from jax.experimental.pallas import tpu as pltpu
from jax.sharding import PartitionSpec as P

RANK = 64
SEQ = 512
WIDTH = 8
STORE = 16
NEAR = 8
MIB = 1024 * 1024


NT = (((1,), (1,)), ((), ()))
NN = (((1,), (0,)), ((), ()))


def split(x):
    high = x.astype(jnp.bfloat16)
    low = (x - high.astype(jnp.float32)).astype(jnp.bfloat16)
    return high, low


def dot(a, b, dims):
    return lax.dot_general(a, b, dims, preferred_element_type=jnp.float32)


def dot3(a, b, dims):
    a_high, a_low = split(a)
    b_high, b_low = split(b)
    return dot(a_high, b_high, dims) + (dot(a_high, b_low, dims) + dot(a_low, b_high, dims))


def limit(mib):
    return pltpu.CompilerParams(vmem_limit_bytes=mib * MIB)


def hbm(x):
    return pltpu.with_memory_space_constraint(x, pltpu.HBM)


VMEM = pl.BlockSpec(memory_space=pltpu.VMEM)
SMEM = pl.BlockSpec(memory_space=pltpu.SMEM)
HBM = pl.BlockSpec(memory_space=pltpu.HBM)


def far_grads_kernel(place_ref, grad_ref, in_ref, out_ref, result_ref, in_held, out_held, tokens, sems):
    copies = [
        pltpu.make_async_copy(source, target, sems.at[i])
        for i, (source, target) in enumerate(
            [(out_ref, out_held)]
            + [(grad_ref.at[place_ref[0] ^ k], tokens.at[i]) for i, k in enumerate(FAR)]
            + [(in_ref, in_held)]
        )
    ]
    for copy in copies:
        copy.start()
    copies[0].wait()
    for i in range(2):
        copies[i + 1].wait()
        result_ref[i * RANK : (i + 1) * RANK, :] = dot(out_held[...], tokens[i], NT)
    copies[3].wait()


def far_grads(place, out_grads, proj_in_t, proj_out_t):
    depth = out_grads.shape[2]
    weight = jax.ShapeDtypeStruct((RANK, depth), jnp.bfloat16)
    return pl.pallas_call(
        far_grads_kernel,
        out_shape=(jax.ShapeDtypeStruct((2 * RANK, SEQ), jnp.float32), weight, weight),
        in_specs=[SMEM, HBM, HBM, HBM],
        out_specs=(VMEM, VMEM, VMEM),
        scratch_shapes=[
            pltpu.VMEM((2, SEQ, depth), jnp.bfloat16),
            pltpu.SemaphoreType.DMA((4,)),
        ],
        compiler_params=limit(6),
        cost_estimate=project_cost(1, depth),
        name="far_grads",
    )(place, hbm(out_grads), hbm(proj_in_t), hbm(proj_out_t))


def far_acts_kernel(place_ref, act_ref, in_ref, result_ref):
    for i, k in enumerate(FAR):
        query = place_ref[0] ^ k
        result_ref[i * RANK : (i + 1) * RANK, :] = dot(in_ref[...], act_ref[query], NT)


def far_acts(place, activations, proj_in_t):
    return pl.pallas_call(
        far_acts_kernel,
        out_shape=jax.ShapeDtypeStruct((2 * RANK, SEQ), jnp.float32),
        in_specs=[SMEM, VMEM, VMEM],
        out_specs=VMEM,
        compiler_params=limit(20),
        cost_estimate=project_cost(1, activations.shape[2]),
        name="far_acts",
    )(place, activations, proj_in_t)


def merge_kernel(side, even_ref, odd_ref, relayed_ref, even_out, odd_out):
    mine = slice(side * RANK, (side + 1) * RANK)
    rest = slice((1 - side) * RANK, (2 - side) * RANK)
    for i, (source, target) in enumerate(((even_ref, even_out), (odd_ref, odd_out))):
        target[rest, :] = source[rest, :]
        target[mine, :] = source[mine, :] + relayed_ref[i * RANK : (i + 1) * RANK, :]


def merge(side, even, odd, relayed):
    part = jax.ShapeDtypeStruct(even.shape, jnp.float32)
    return pl.pallas_call(
        functools.partial(merge_kernel, side),
        out_shape=(part, part),
        in_specs=[VMEM] * 3,
        out_specs=(VMEM, VMEM),
        compiler_params=limit(4),
        name="merge",
    )(even, odd, relayed)


def project_cost(count, depth):
    return pl.CostEstimate(
        flops=4 * count * SEQ * depth * RANK,
        bytes_accessed=4 * count * SEQ * depth,
        transcendentals=0,
    )


def project_kernel(group, place_ref, act_ref, grad_ref, in_ref, out_ref, *result_refs):
    for k, result_ref in zip(group, result_refs, strict=True):
        query = place_ref[0] ^ k
        result_ref[:RANK, :] = dot(out_ref[...], grad_ref[query], NT)
        result_ref[RANK:, :] = dot(in_ref[...], act_ref[query], NT)


def project(group, place, activations, out_grads, proj_in_t, proj_out_t):
    count = len(group)
    part = jax.ShapeDtypeStruct((2 * RANK, SEQ), jnp.float32)
    return pl.pallas_call(
        functools.partial(project_kernel, group),
        out_shape=(part,) * count,
        in_specs=[SMEM, VMEM, VMEM, VMEM, VMEM],
        out_specs=(VMEM,) * count,
        compiler_params=limit(20),
        cost_estimate=project_cost(count, activations.shape[2]),
        name="project",
    )(place, activations, out_grads, proj_in_t, proj_out_t)


def gradient_kernel(place_ref, *refs):
    *parts, result_ref, held = refs
    total = parts[0][...]
    for part in parts[1:]:
        total = total + part[...]
    held[...] = dot3(total[:RANK], total[RANK:], NT) * (1.0 / SEQ)
    half = RANK // 2
    pairs = jnp.concatenate(
        [held[pl.ds(0, half, stride=2), :], held[pl.ds(1, half, stride=2), :]], axis=1
    )
    row = lax.broadcasted_iota(jnp.int32, pairs.shape, 0)
    for bit in (1, 2, 4):
        far = 2 * bit
        swapped = jnp.where(
            (row & far) == 0, pltpu.roll(pairs, half - far, 0), pltpu.roll(pairs, far, 0)
        )
        pairs = jnp.where((place_ref[1] & bit) != 0, swapped, pairs)
    for side in range(2):
        block = pairs[side * 16 : (side + 1) * 16, :]
        for i in range(WIDTH):
            result_ref[side * WIDTH + i] = block


def gradient(place, parts):
    return pl.pallas_call(
        gradient_kernel,
        out_shape=jax.ShapeDtypeStruct((2 * WIDTH, 16, 128), jnp.float32),
        in_specs=[SMEM] + [VMEM] * len(parts),
        out_specs=VMEM,
        scratch_shapes=[pltpu.VMEM((RANK, RANK), jnp.float32)],
        compiler_params=limit(4),
        name="gradient",
    )(place, *parts)


def partial_kernel(rows_ref, *refs):
    *fisher_refs, result_ref = refs
    total = None
    for i, fisher_ref in enumerate(fisher_refs):
        rows = jnp.concatenate([rows_ref[:, 2 * i, :], rows_ref[:, 2 * i + 1, :]], axis=1)
        high, low = split(rows)
        f_high, f_low = split(fisher_ref[...])
        half = rows.shape[0]
        wide = dot(jnp.concatenate([high, low], axis=0), f_high, NN)
        term = wide[:half] + (wide[half:] + dot(high, f_low, NN))
        total = term if total is None else total + term
    for i in range(STORE // 2):
        result_ref[i] = total


def partial_precond(rows, fisher):
    columns = fisher[0].shape[1]
    return pl.pallas_call(
        partial_kernel,
        out_shape=jax.ShapeDtypeStruct((STORE // 2, 2 * WIDTH, columns), jnp.float32),
        in_specs=[VMEM] * (1 + len(fisher)),
        out_specs=VMEM,
        compiler_params=limit(10),
        name="partial_precond",
    )(rows, *fisher)


def split_kernel(store_ref, high_ref, low_ref):
    high_ref[...], low_ref[...] = split(store_ref[...])


def split_store(store):
    half = jax.ShapeDtypeStruct(store.shape, jnp.bfloat16)
    return pl.pallas_call(
        split_kernel,
        out_shape=(half, half),
        in_specs=[VMEM],
        out_specs=(VMEM, VMEM),
        compiler_params=limit(12),
        name="split_store",
    )(store)


def score_kernel(place_ref, own_ref, other_ref, high_ref, low_ref, *refs):
    *result_refs, parts = refs
    rows = 8
    half = 2 * WIDTH * rows
    for k in range(WIDTH):
        owner = place_ref[0] ^ k
        z = owner & 3
        offset = pl.ds(pl.multiple_of((owner >> 2) * rows, rows), rows)
        for swap, halves_ref in enumerate((own_ref, other_ref)):
            core = (place_ref[1] & 1) ^ swap
            block = halves_ref[z, offset, :] + halves_ref[4 + z, offset, :]
            start = pl.multiple_of((2 * k + core) * rows, rows)
            high = block.astype(jnp.bfloat16).astype(jnp.float32)
            parts[pl.ds(start, rows), :] = high
            parts[pl.ds(start + half, rows), :] = block - high
    both = parts[...].astype(jnp.bfloat16)
    width = 2048
    for n in range(high_ref.shape[0] // width):
        span = slice(n * width, (n + 1) * width)
        wide = dot(both, high_ref[span, :], NT)
        total = wide[:half] + (wide[half:] + dot(both[:half], low_ref[span, :], NT))
        for k in range(WIDTH):
            result_refs[k][:, span] = total[16 * k : 16 * (k + 1), :]


def scores(place, own, other, high, low):
    examples, columns = high.shape
    block = jax.ShapeDtypeStruct((16, examples), jnp.float32)
    return pl.pallas_call(
        score_kernel,
        out_shape=(block,) * WIDTH,
        in_specs=[SMEM, VMEM, VMEM, VMEM, VMEM],
        out_specs=(VMEM,) * WIDTH,
        scratch_shapes=[pltpu.VMEM((256, columns), jnp.float32)],
        compiler_params=limit(12),
        name="scores",
    )(place, own, other, high, low)


def exchange(x, axis, k, size):
    return lax.ppermute(x, axis, [(i, i ^ k) for i in range(size)])


ORDER = (2, 6, 5, 4, 3, 7, 1)
FAR = (4, 5)


def body(activations, out_grads, proj_in, proj_out, fisher_inv, grad_store):
    place = jnp.stack([lax.axis_index("width"), lax.axis_index("store") & (NEAR - 1)])
    proj_in_t, proj_out_t = proj_in.T, proj_out.T
    parts, fisher = {}, {0: fisher_inv}

    def send(part, k):
        return exchange(part, "width", k, WIDTH)

    grads, proj_in_t, proj_out_t = far_grads(place, out_grads, proj_in_t, proj_out_t)
    weights = (activations, out_grads, proj_in_t, proj_out_t)
    grads = send(grads, 2)
    acts = far_acts(place, activations, proj_in_t)
    acts = send(acts, 6)
    for k in (4, 2, 6):
        fisher[k] = exchange(fisher_inv, "store", k, STORE)
    (beside,) = project((1,), place, *weights)
    parts[1] = send(beside, 1)
    near = dict(zip((6, 7, 2, 3), project((6, 7, 2, 3), place, *weights), strict=True))
    near[6], near[7] = merge(0, near[6], near[7], grads)
    near[2], near[3] = merge(1, near[2], near[3], acts)
    for k in (7, 6, 3, 2):
        parts[k] = send(near[k], k)
    (parts[0],) = project((0,), place, *weights)
    last, *blocks = lax.optimization_barrier((parts[0], *(fisher[k] for k in (0, 2, 4, 6))))
    for k, block in zip((0, 2, 4, 6), blocks, strict=True):
        fisher[k + 1] = exchange(block, "store", 1, STORE)
    store, _ = lax.optimization_barrier((grad_store, parts[0]))
    high, low = split_store(store)
    outgoing = gradient(place, list(parts.values()))
    groups = [
        [(side * NEAR + i) * WIDTH + w for side in range(2) for w in range(WIDTH)]
        for i in range(NEAR)
    ]
    rows = lax.all_to_all(outgoing, ("store", "width"), 0, 0, axis_index_groups=groups)
    halves = partial_precond(rows, [fisher[i] for i in range(NEAR)])
    cores = [list(range(core, STORE, 2)) for core in range(2)]
    halves = lax.all_to_all(halves, "store", 0, 0, axis_index_groups=cores)
    blocks = scores(place, halves, exchange(halves, "store", 1, STORE), high, low)
    total = blocks[0]
    for block in [exchange(blocks[k], "width", k, WIDTH) for k in ORDER]:
        total = total + block
    return total


def solution(mesh):
    placed = (
        P("store", None, "width"),
        P("store", None, "width"),
        P("width", None),
        P("width", None),
        P("store", "width"),
        P("store", "width"),
    )
    return jax.shard_map(
        body, mesh=mesh, in_specs=placed, out_specs=P("width", "store"), check_vma=False
    )
```
